512 devices in a mesh: aux: 32 (over x_lo, y, core), pair: 16 (over z, x_hi).
Axes of the slice: x: 4 (x_hi: 2, x_lo: 2; x = x_hi * 2 + x_lo), y: 8, z: 8, core: 2. Of those that a mesh axis runs over, the one named last changes fastest.
Arguments:
- integrals: bfloat16 [4096, 32, 512], P('aux', 'pair'), may hold values from -0.5 to 0.5
- occ_density: bfloat16 [32, 32], replicated, may hold values from -1 to 1
- virt_density: bfloat16 [512, 512], replicated, may hold values from -0.25 to 0.25
- screen: int32 [64, 32], P('aux', 'pair'), may hold values 0 or 1
Outputs:
- polar: float32 [4096, 4096], P('aux', 'pair')
The draws below stay inside these ranges and needn't reach their ends.
All inputs are finite; a program needn't handle non-finite values. No bound on the sum of `screen` on one device may be relied on, other than what follows from the above.
Results may differ from the reference program's by a relative error of at most 0.0041.
Values may be sent and summed in bfloat16 or wider, within the bound.
No kernel may reach another device: no remote copies, remote signals or barrier semaphores. Data moves between devices by JAX's collectives and lax.ppermute only.
A program may use at most 64 MiB of HBM per device.

```python
import jax
import jax.numpy as jnp

ORB = 512
BLK = 64
MU = 32
AUX = 4096


def plant(values, rng, low, high):
    shape = values.shape
    spot = [jax.random.randint(jax.random.fold_in(rng, axis), (), 0, shape[axis]) for axis in range(len(shape))]
    values = values.at[tuple(spot)].set(low)
    longest = shape.index(max(shape))
    spot[longest] = (spot[longest] + 1) % shape[longest]
    return values.at[tuple(spot)].set(high)


def block_levels(own_key, extent, pieces, low, top_value):
    def one(position, shards_of):
        draws = jax.random.uniform(jax.random.fold_in(jax.random.fold_in(own_key, 6), position), (shards_of,), jnp.float32, low / len(pieces), top_value / len(pieces))
        return jnp.repeat(jnp.exp(draws), extent[position] // shards_of).reshape((-1,) + (1,) * (len(extent) - position - 1))

    gain = one(*pieces[0])
    for cut in pieces[1:]:
        gain = gain * one(*cut)
    return gain


def scatter_about(own_key, shape, deviation, bound, pieces=(), kind=jnp.bfloat16):
    values = jax.random.normal(own_key, shape, jnp.float32) * deviation
    if len(pieces) > 0:
        values = block_levels(own_key, shape, pieces, -0.22, 0.18) * values
    return jnp.clip(values, min=-bound, max=bound).astype(kind)


def setup_inputs(seed: int = 0) -> dict:
    key_list = jax.random.split(jax.random.key(seed), 5)
    return {
        "integrals": scatter_about(key_list[0], (AUX, MU, ORB), 0.09, 0.5, ((0, 32), (1, 16))),
        "occ_density": scatter_about(key_list[1], (MU, MU), MU ** -0.5, 1.0),
        "virt_density": scatter_about(key_list[2], (ORB, ORB), ORB ** -0.5, 0.25),
        "screen": plant((jax.random.randint(key_list[3], (AUX // BLK, MU), 0, 4) < 3).astype(jnp.int32), jax.random.fold_in(key_list[3], 1), 0, 1),
    }


def reference(integrals, occ_density, virt_density, screen):
    aux_rows, mu_count, orbitals = integrals.shape
    blocks = screen.shape[0]
    grouped = integrals.reshape(blocks, aux_rows // blocks, mu_count, orbitals)
    screened = jnp.where(screen[:, None, :, None] > 0, grouped, jnp.zeros_like(grouped)).reshape(aux_rows, mu_count, orbitals)
    virtual_sec = jnp.dot(screened.reshape(aux_rows * mu_count, orbitals), virt_density, preferred_element_type=jnp.float32)
    virtual_sec = virtual_sec.astype(jnp.bfloat16).reshape(aux_rows, mu_count, orbitals)
    occupied = jnp.einsum("pms,ml->pls", virtual_sec.astype(jnp.float32), occ_density.astype(jnp.float32)).astype(jnp.bfloat16)
    polar = jnp.dot(occupied.reshape(aux_rows, mu_count * orbitals), screened.reshape(aux_rows, mu_count * orbitals).T, preferred_element_type=jnp.float32)
    return polar
```

```python
import jax
import jax.numpy as jnp
from jax import lax
from jax.sharding import Mesh, PartitionSpec as P

AUX = ("x_lo", "y", "core")
PAIR = ("z", "x_hi")
PLANE = ("x_lo", "core", "z", "x_hi")
WIDE = ("x_lo", "core", "x_hi")


def exchange(values):
    pieces = values.reshape(2, 2, 2, 16, 2, 8, 64)
    pieces = pieces.transpose(0, 1, 5, 2, 3, 4, 6).reshape(64, 16, 128)
    got = lax.all_to_all(pieces, PLANE, 0, 0, tiled=True)
    got = got.reshape(4, 16, 16, 128).transpose(0, 2, 1, 3)
    return got.reshape(64, 2048)


def body(integrals, occ_density, virt_density, screen):
    aux_rows, local_pairs, orbitals = integrals.shape
    blocks = screen.shape[0]
    grouped = integrals.reshape(blocks, aux_rows // blocks, local_pairs, orbitals)
    screened = jnp.where(screen[:, None, :, None] > 0, grouped, jnp.zeros_like(grouped)).reshape(
        aux_rows, local_pairs, orbitals
    )
    virtual = jnp.dot(
        screened.reshape(aux_rows * local_pairs, orbitals),
        virt_density,
        preferred_element_type=jnp.float32,
    ).astype(jnp.bfloat16).reshape(aux_rows, local_pairs, orbitals)
    mine = exchange(screened)
    columns = lax.all_gather(mine, "y", axis=0, tiled=True)
    virt_rows = exchange(virtual).reshape(64, 32, 64)
    occupied = jnp.einsum("pms,ml->pls", virt_rows, occ_density, preferred_element_type=jnp.float32)
    occupied = occupied.astype(jnp.bfloat16).reshape(64, 2048)
    rows = lax.all_gather(occupied, WIDE, axis=0, tiled=True)
    rows = rows.reshape(8, 4, 16, 2048).transpose(1, 0, 2, 3).reshape(512, 2048)
    part = lax.dot_general(columns, rows, (((1,), (1,)), ((), ())), preferred_element_type=jnp.float32)
    part = part.astype(jnp.bfloat16)
    tiles = part.reshape(4, 2, 2, 32, 2, 2, 128).transpose(4, 5, 2, 0, 1, 3, 6).reshape(64, 32, 128)
    got = lax.all_to_all(tiles, PLANE, 0, 0, tiled=True)
    total = jnp.sum(got.reshape(2, 2, 8, 2, 2, 16, 128).astype(jnp.float32), axis=2)
    return total.transpose(5, 3, 0, 1, 2, 4).reshape(128, 256)


def solution(mesh):
    fine = Mesh(mesh.devices.reshape(2, 8, 2, 8, 2), AUX + PAIR)
    placed = (P(AUX, PAIR, None), P(), P(), P(AUX, PAIR))
    return jax.shard_map(body, mesh=fine, in_specs=placed, out_specs=P(AUX, PAIR), check_vma=False)
```

```python
import jax
import jax.numpy as jnp
from jax import lax
from jax.experimental import pallas as pl
from jax.experimental.pallas import tpu as pltpu
from jax.sharding import Mesh, PartitionSpec as P

AUX = ("x_lo", "y", "core")
PAIR = ("z", "x_hi")
PLANE = ("x_lo", "core", "z", "x_hi")
WIDE = ("x_lo", "core", "x_hi")


def y_hop(first):
    pairs = []
    for y in range(8):
        for core in range(2):
            step = 1 if (core == 0) == first else -1
            pairs.append((y * 2 + core, (y + step) % 8 * 2 + core))
    return pairs


def wide_index(place, core):
    return place % 2 * 4 + core * 2 + place // 2


def x_hop(first):
    pairs = []
    for place in range(4):
        for core in range(2):
            step = 1 if (core == 0) == first else -1
            pairs.append((wide_index(place, core), wide_index((place + step) % 4, core)))
    return pairs


def pack(values):
    pieces = values.reshape(2, 2, 2, 16, 2, 8, 64)
    return pieces.transpose(0, 1, 5, 2, 3, 4, 6).reshape(64, 16, 128)


def unpack(got):
    return got.reshape(4, 16, 16, 128).transpose(0, 2, 1, 3).reshape(64, 2048)


def multiply_kernel(where_ref, *refs):
    columns, mine, other, (out_ref, left, right) = refs[:8], refs[8:12], refs[12], refs[13:]
    y, place, core = where_ref[0], where_ref[1], where_ref[2]
    sign = 1 - 2 * core
    for i, steps in enumerate((0, 1, 2, 3, 4, -3, -2, -1)):
        at = lax.rem(y - sign * steps + 8, 8)
        left[pl.ds(pl.multiple_of(at * 64, 64), 64), :] = columns[i][...]
    for i, steps in enumerate((0, 1, 2, -1)):
        for near in range(2):
            step = sign * steps if near else -sign * steps
            source = lax.rem(place - step + 8, 4)
            owner = core if near else 1 - core
            at = lax.rem(source, 2) * 4 + owner * 2 + source // 2
            for group in range(4):
                piece = pl.ds(group * 16, 16)
                value = mine[i][piece, :] if near else other[i, piece, :]
                right[pl.ds(pl.multiple_of(group * 128 + at * 16, 16), 16), :] = value
    for y_column in range(8):
        for half in range(1):
            part = lax.dot_general(
                left[y_column * 64 : y_column * 64 + 64, :],
                right[...],
                (((1,), (1,)), ((), ())),
                preferred_element_type=jnp.float32,
            ).astype(jnp.bfloat16)
            for x_lo_q in range(2):
                for group in range(4):
                    dest = group * 16 + (x_lo_q * 4 + y_column // 2) * 2 + y_column % 2
                    out_ref[dest] = part[x_lo_q * 32 : x_lo_q * 32 + 32, group * 128 : group * 128 + 128]


def multiply(where, columns, mine, other):
    vmem = pl.BlockSpec(memory_space=pltpu.VMEM)
    return pl.pallas_call(
        multiply_kernel,
        out_shape=jax.ShapeDtypeStruct((64, 32, 128), jnp.bfloat16),
        in_specs=[pl.BlockSpec(memory_space=pltpu.SMEM)] + [vmem] * 13,
        out_specs=vmem,
        scratch_shapes=[pltpu.VMEM((512, 2048), jnp.bfloat16), pltpu.VMEM((512, 2048), jnp.bfloat16)],
        compiler_params=pltpu.CompilerParams(vmem_limit_bytes=32 * 1024 * 1024),
    )(where, *columns, *mine, other)


def body(integrals, occ_density, virt_density, screen):
    aux_rows, local_pairs, orbitals = integrals.shape
    blocks = screen.shape[0]
    grouped = integrals.reshape(blocks, aux_rows // blocks, local_pairs, orbitals)
    screened = jnp.where(screen[:, None, :, None] > 0, grouped, jnp.zeros_like(grouped)).reshape(
        aux_rows, local_pairs, orbitals
    )
    virtual = jnp.dot(
        screened.reshape(aux_rows * local_pairs, orbitals),
        virt_density,
        preferred_element_type=jnp.float32,
    ).astype(jnp.bfloat16).reshape(aux_rows, local_pairs, orbitals)
    both = jnp.concatenate([pack(screened), pack(virtual)], axis=1)
    got = lax.all_to_all(both, PLANE, 0, 0, tiled=True)
    own = unpack(got[:, :16])
    ahead, behind = [own], [own]
    for step in range(3):
        ahead.append(lax.ppermute(ahead[-1], ("y", "core"), y_hop(True)))
        behind.append(lax.ppermute(behind[-1], ("y", "core"), y_hop(False)))
    ahead.append(lax.ppermute(ahead[-1], ("y", "core"), y_hop(True)))
    columns = ahead + behind[:0:-1]
    virt_rows = unpack(got[:, 16:]).reshape(64, 32, 64)
    occupied = jnp.einsum("pms,ml->pls", virt_rows, occ_density, preferred_element_type=jnp.float32)
    occupied = occupied.astype(jnp.bfloat16).reshape(64, 2048)
    near = lax.ppermute(occupied, WIDE, x_hop(True))
    back = lax.ppermute(occupied, WIDE, x_hop(False))
    far = lax.ppermute(near, WIDE, x_hop(True))
    mine = [occupied, near, far, back]
    other = lax.ppermute(jnp.stack(mine), "core", [(0, 1), (1, 0)])
    place = lax.axis_index("x_hi") * 2 + lax.axis_index("x_lo")
    where = jnp.stack([lax.axis_index("y"), place, lax.axis_index("core")]).astype(jnp.int32)
    tiles = multiply(where, columns, mine, other)
    got = lax.all_to_all(tiles, PLANE, 0, 0, tiled=True)
    total = jnp.sum(got.reshape(2, 2, 8, 2, 2, 16, 128).astype(jnp.float32), axis=2)
    return total.transpose(5, 3, 0, 1, 2, 4).reshape(128, 256)


def solution(mesh):
    fine = Mesh(mesh.devices.reshape(2, 8, 2, 8, 2), AUX + PAIR)
    placed = (P(AUX, PAIR, None), P(), P(), P(AUX, PAIR))
    return jax.shard_map(body, mesh=fine, in_specs=placed, out_specs=P(AUX, PAIR), check_vma=False)
```

```python
import jax
import jax.numpy as jnp
from jax import lax
from jax.experimental import pallas as pl
from jax.experimental.pallas import tpu as pltpu
from jax.sharding import Mesh, PartitionSpec as P

AUX = ("x_lo", "y", "core")
PAIR = ("z", "x_hi")
PLANE = ("x_lo", "core", "z", "x_hi")
WIDE = ("x_lo", "core", "x_hi")


def wide_index(place, core):
    return place % 2 * 4 + core * 2 + place // 2


def x_hop(first):
    pairs = []
    for place in range(4):
        for core in range(2):
            step = 1 if (core == 0) == first else -1
            pairs.append((wide_index(place, core), wide_index((place + step) % 4, core)))
    return pairs


def pack(values):
    pieces = values.reshape(2, 2, 2, 16, 2, 8, 64)
    return pieces.transpose(0, 1, 5, 2, 3, 4, 6).reshape(64, 16, 128)


def unpack(got):
    return got.reshape(4, 16, 16, 128).transpose(0, 2, 1, 3).reshape(64, 2048)


def multiply_kernel(where_ref, columns_ref, *refs):
    mine, other, (out_ref, right) = refs[:4], refs[4], refs[5:]
    place, core = where_ref[0], where_ref[1]
    part_id = pl.program_id(0)

    @pl.when(part_id == 0)
    def _():
        sign = 1 - 2 * core
        for i, steps in enumerate((0, 1, 2, -1)):
            for near in range(2):
                step = sign * steps if near else -sign * steps
                source = lax.rem(place - step + 8, 4)
                owner = core if near else 1 - core
                at = lax.rem(source, 2) * 4 + owner * 2 + source // 2
                for group in range(4):
                    piece = pl.ds(group * 16, 16)
                    value = mine[i][piece, :] if near else other[i, piece, :]
                    right[pl.ds(pl.multiple_of(group * 128 + at * 16, 16), 16), :] = value

    part = lax.dot_general(
        columns_ref[...], right[...], (((1,), (1,)), ((), ())), preferred_element_type=jnp.float32
    ).astype(jnp.bfloat16)
    for y_column in range(4):
        for x_lo_q in range(2):
            for group in range(4):
                row = y_column * 64 + x_lo_q * 32
                dest = group * 16 + (x_lo_q * 4 + part_id * 2 + y_column // 2) * 2 + y_column % 2
                out_ref[dest] = part[row : row + 32, group * 128 : group * 128 + 128]


def multiply(where, columns, mine, other):
    vmem = pl.BlockSpec(memory_space=pltpu.VMEM)
    return pl.pallas_call(
        multiply_kernel,
        out_shape=jax.ShapeDtypeStruct((64, 32, 128), jnp.bfloat16),
        grid=(2,),
        in_specs=[pl.BlockSpec(memory_space=pltpu.SMEM), pl.BlockSpec((256, 2048), lambda i: (i, 0))] + [vmem] * 5,
        out_specs=vmem,
        scratch_shapes=[pltpu.VMEM((512, 2048), jnp.bfloat16)],
        compiler_params=pltpu.CompilerParams(vmem_limit_bytes=24 * 1024 * 1024),
    )(where, columns, *mine, other)


def body(integrals, occ_density, virt_density, screen):
    aux_rows, local_pairs, orbitals = integrals.shape
    blocks = screen.shape[0]
    grouped = integrals.reshape(blocks, aux_rows // blocks, local_pairs, orbitals)
    screened = jnp.where(screen[:, None, :, None] > 0, grouped, jnp.zeros_like(grouped)).reshape(
        aux_rows, local_pairs, orbitals
    )
    virtual = jnp.dot(
        screened.reshape(aux_rows * local_pairs, orbitals),
        virt_density,
        preferred_element_type=jnp.float32,
    ).astype(jnp.bfloat16).reshape(aux_rows, local_pairs, orbitals)
    both = jnp.concatenate([pack(screened), pack(virtual)], axis=1)
    got = lax.all_to_all(both, PLANE, 0, 0, tiled=True)
    own = unpack(got[:, :16])
    columns = lax.all_gather(own, "y", axis=0, tiled=True)
    virt_rows = unpack(got[:, 16:]).reshape(64, 32, 64)
    occupied = jnp.einsum("pms,ml->pls", virt_rows, occ_density, preferred_element_type=jnp.float32)
    occupied = occupied.astype(jnp.bfloat16).reshape(64, 2048)
    near = lax.ppermute(occupied, WIDE, x_hop(True))
    back = lax.ppermute(occupied, WIDE, x_hop(False))
    far = lax.ppermute(near, WIDE, x_hop(True))
    mine = [occupied, near, far, back]
    other = lax.ppermute(jnp.stack(mine), "core", [(0, 1), (1, 0)])
    place = lax.axis_index("x_hi") * 2 + lax.axis_index("x_lo")
    where = jnp.stack([place, lax.axis_index("core")]).astype(jnp.int32)
    tiles = multiply(where, columns, mine, other)
    got = lax.all_to_all(tiles, PLANE, 0, 0, tiled=True)
    total = jnp.sum(got.reshape(2, 2, 8, 2, 2, 16, 128).astype(jnp.float32), axis=2)
    return total.transpose(5, 3, 0, 1, 2, 4).reshape(128, 256)


def solution(mesh):
    fine = Mesh(mesh.devices.reshape(2, 8, 2, 8, 2), AUX + PAIR)
    placed = (P(AUX, PAIR, None), P(), P(), P(AUX, PAIR))
    return jax.shard_map(body, mesh=fine, in_specs=placed, out_specs=P(AUX, PAIR), check_vma=False)
```

```python
import jax
import jax.numpy as jnp
from jax import lax
from jax.experimental import pallas as pl
from jax.experimental.pallas import tpu as pltpu
from jax.sharding import Mesh, PartitionSpec as P


AUX = ("x_lo", "y", "core")
PAIR = ("z", "x_hi")
PLANE = ("x_lo", "core", "z", "x_hi")
WIDE = ("x_lo", "core", "x_hi")


def ring(step):
    return [(y, (y + step) % 8) for y in range(8)]


def wide_index(place, core):
    return place % 2 * 4 + core * 2 + place // 2


def x_hop(first):
    pairs = []
    for place in range(4):
        for core in range(2):
            step = 1 if (core == 0) == first else -1
            pairs.append((wide_index(place, core), wide_index((place + step) % 4, core)))
    return pairs


def pack(values):
    pieces = values.reshape(2, 2, 2, 16, 2, 8, 64)
    return pieces.transpose(0, 1, 5, 2, 3, 4, 6).reshape(64, 16, 128)


def unpack(got):
    return got.reshape(4, 16, 16, 128).transpose(0, 2, 1, 3).reshape(64, 2048)


def multiply_kernel(where_ref, *refs):
    columns, mine, other, (out_ref, left, right, done) = refs[:9], refs[9:13], refs[13], refs[14:]
    y, place, core = where_ref[0], where_ref[1], where_ref[2]
    copies = []

    def bring(source, target):
        copies.append(pltpu.make_async_copy(source, target, done.at[len(copies)]))
        copies[-1].start()

    for i, steps in enumerate((0, 1, 2, 3, -1, -2, -3)):
        at = lax.rem(y - steps + 8, 8)
        bring(columns[i], left.at[pl.ds(pl.multiple_of(at * 64, 64), 64), :])
    at = lax.rem(y + 4, 8)
    bring(columns[7], left.at[pl.ds(pl.multiple_of(at * 64, 32), 32), :])
    bring(columns[8], left.at[pl.ds(pl.multiple_of(at * 64 + 32, 32), 32), :])
    sign = 1 - 2 * core
    for i, steps in enumerate((0, 1, 2, -1)):
        for near in range(2):
            step = sign * steps if near else -sign * steps
            source = lax.rem(place - step + 8, 4)
            owner = core if near else 1 - core
            at = lax.rem(source, 2) * 4 + owner * 2 + source // 2
            bring(mine[i] if near else other.at[i], right.at[:, pl.ds(pl.multiple_of(at * 16, 16), 16), :])
    for copy in copies:
        copy.wait()
    for part_id in range(2):
        part = lax.dot_general(
            left[part_id * 256 : part_id * 256 + 256, :],
            right[...].reshape(512, 2048),
            (((1,), (1,)), ((), ())),
            preferred_element_type=jnp.float32,
        ).astype(jnp.bfloat16)
        for y_column in range(4):
            for x_lo_q in range(2):
                for group in range(4):
                    row = y_column * 64 + x_lo_q * 32
                    dest = group * 16 + (x_lo_q * 4 + part_id * 2 + y_column // 2) * 2 + y_column % 2
                    out_ref[dest] = part[row : row + 32, group * 128 : group * 128 + 128]


def multiply(where, columns, mine, other):
    mine = [block.reshape(4, 16, 2048) for block in mine]
    return pl.pallas_call(
        multiply_kernel,
        out_shape=jax.ShapeDtypeStruct((64, 32, 128), jnp.bfloat16),
        in_specs=[pl.BlockSpec(memory_space=pltpu.SMEM)] + [pl.BlockSpec(memory_space=pl.ANY)] * 14,
        out_specs=pl.BlockSpec(memory_space=pltpu.VMEM),
        scratch_shapes=[
            pltpu.VMEM((512, 2048), jnp.bfloat16),
            pltpu.VMEM((4, 128, 2048), jnp.bfloat16),
            pltpu.SemaphoreType.DMA((17,)),
        ],
        compiler_params=pltpu.CompilerParams(vmem_limit_bytes=16 * 1024 * 1024),
        cost_estimate=pl.CostEstimate(flops=2 * 512 * 512 * 2048, bytes_accessed=4 << 20, transcendentals=0),
    )(where, *columns, *mine, other.reshape(4, 4, 16, 2048))


def body(integrals, occ_density, virt_density, screen):
    aux_rows, local_pairs, orbitals = integrals.shape
    blocks = screen.shape[0]
    grouped = integrals.reshape(blocks, aux_rows // blocks, local_pairs, orbitals)
    screened = jnp.where(screen[:, None, :, None] > 0, grouped, jnp.zeros_like(grouped)).reshape(
        aux_rows, local_pairs, orbitals
    )
    virtual = jnp.dot(
        screened.reshape(aux_rows * local_pairs, orbitals),
        virt_density,
        preferred_element_type=jnp.float32,
    ).astype(jnp.bfloat16).reshape(aux_rows, local_pairs, orbitals)
    both = jnp.concatenate([pack(screened), pack(virtual)], axis=1)
    got = lax.all_to_all(both, PLANE, 0, 0, tiled=True)
    own = unpack(got[:, :16])
    up1 = lax.ppermute(own, "y", ring(1))
    down1 = lax.ppermute(own, "y", ring(-1))
    up2 = lax.ppermute(up1, "y", ring(1))
    down2 = lax.ppermute(down1, "y", ring(-1))
    up3 = lax.ppermute(up2, "y", ring(1))
    down3 = lax.ppermute(down2, "y", ring(-1))
    up4 = lax.ppermute(up3[:32], "y", ring(1))
    down4 = lax.ppermute(down3[32:], "y", ring(-1))
    columns = [own, up1, up2, up3, down1, down2, down3, up4, down4]
    virt_rows = unpack(got[:, 16:]).reshape(64, 32, 64)
    occupied = jnp.einsum("pms,ml->pls", virt_rows, occ_density, preferred_element_type=jnp.float32)
    occupied = occupied.astype(jnp.bfloat16).reshape(64, 2048)
    near = lax.ppermute(occupied, WIDE, x_hop(True))
    back = lax.ppermute(occupied, WIDE, x_hop(False))
    far = lax.ppermute(near, WIDE, x_hop(True))
    mine = [occupied, near, far, back]
    other = lax.ppermute(jnp.stack(mine), "core", [(0, 1), (1, 0)])
    place = lax.axis_index("x_hi") * 2 + lax.axis_index("x_lo")
    where = jnp.stack([lax.axis_index("y"), place, lax.axis_index("core")]).astype(jnp.int32)
    tiles = multiply(where, columns, mine, other)
    got = lax.all_to_all(tiles, PLANE, 0, 0, tiled=True)
    total = jnp.sum(got.reshape(2, 2, 8, 2, 2, 16, 128).astype(jnp.float32), axis=2)
    return total.transpose(5, 3, 0, 1, 2, 4).reshape(128, 256)


def solution(mesh):
    fine = Mesh(mesh.devices.reshape(2, 8, 2, 8, 2), AUX + PAIR)
    placed = (P(AUX, PAIR, None), P(), P(), P(AUX, PAIR))

    return jax.shard_map(body, mesh=fine, in_specs=placed, out_specs=P(AUX, PAIR), check_vma=False)
```

```python
import jax
import jax.numpy as jnp
from jax import lax
from jax.experimental import pallas as pl
from jax.experimental.pallas import tpu as pltpu
from jax.sharding import Mesh, PartitionSpec as P


AUX = ("x_lo", "y_hi", "y_lo", "core")
PAIR = ("z", "x_hi")
GROUP = ("x_lo", "y_lo", "core", "z", "x_hi")
WIDE = ("x_lo", "core", "x_hi")
TALL = ("y_hi", "core")


def ring(step):
    return [(y, (y + step) % 4) for y in range(4)]


def y_hop():
    return [(y * 2 + core, (y + 1 - 2 * core) % 4 * 2 + core) for y in range(4) for core in range(2)]


def wide_index(place, core):
    return place % 2 * 4 + core * 2 + place // 2


def x_hop(first):
    pairs = []
    for place in range(4):
        for core in range(2):
            step = 1 if (core == 0) == first else -1
            pairs.append((wide_index(place, core), wide_index((place + step) % 4, core)))
    return pairs


def pack(both):
    pieces = both.reshape(2, 2, 2, 2, 16, 2, 8, 2, 32)
    return pieces.transpose(1, 7, 2, 6, 3, 4, 0, 5, 8).reshape(128, 16, 128)


def unpack(got):
    return got.reshape(8, 16, 16, 64).transpose(0, 2, 1, 3).reshape(128, 1024)


def multiply_kernel(where_ref, *refs):
    columns, mine, other, (out_ref, left, right, done) = refs[:4], refs[4:8], refs[8], refs[9:]
    y, place, core = where_ref[0], where_ref[1], where_ref[2]
    copies = []

    def bring(source, target):
        copies.append(pltpu.make_async_copy(source, target, done.at[len(copies)]))
        copies[-1].start()

    for i, steps in enumerate((0, 1, -1, 2)):
        at = lax.rem(y - steps + 4, 4)
        bring(columns[i], left.at[pl.ds(pl.multiple_of(at * 128, 128), 128), :])
    sign = 1 - 2 * core
    for i, steps in enumerate((0, 1, 2, -1)):
        for near in range(2):
            step = sign * steps if near else -sign * steps
            source = lax.rem(place - step + 8, 4)
            owner = core if near else 1 - core
            at = lax.rem(source, 2) * 4 + owner * 2 + source // 2
            bring(mine[i] if near else other.at[i], right.at[:, pl.ds(pl.multiple_of(at * 16, 16), 16), :])
    for copy in copies:
        copy.wait()
    for part_id in range(4):
        part = lax.dot_general(
            left[part_id * 128 : part_id * 128 + 128, :],
            right[...].reshape(1024, 1024),
            (((1,), (1,)), ((), ())),
            preferred_element_type=jnp.float32,
        ).astype(jnp.bfloat16)
        for x_lo_q in range(2):
            for y_lo_q in range(2):
                for group in range(8):
                    row = x_lo_q * 64 + y_lo_q * 32
                    dest = group * 16 + (x_lo_q * 4 + part_id) * 2 + y_lo_q
                    out_ref[dest] = part[row : row + 32, group * 128 : group * 128 + 128]


def multiply(where, columns, mine, other):
    mine = [block.reshape(8, 16, 1024) for block in mine]
    return pl.pallas_call(
        multiply_kernel,
        out_shape=jax.ShapeDtypeStruct((128, 32, 128), jnp.bfloat16),
        in_specs=[pl.BlockSpec(memory_space=pltpu.SMEM)] + [pl.BlockSpec(memory_space=pl.ANY)] * 9,
        out_specs=pl.BlockSpec(memory_space=pltpu.VMEM),
        scratch_shapes=[
            pltpu.VMEM((512, 1024), jnp.bfloat16),
            pltpu.VMEM((8, 128, 1024), jnp.bfloat16),
            pltpu.SemaphoreType.DMA((12,)),
        ],
        compiler_params=pltpu.CompilerParams(vmem_limit_bytes=16 * 1024 * 1024),
        cost_estimate=pl.CostEstimate(flops=2 * 512 * 1024 * 1024, bytes_accessed=4 << 20, transcendentals=0),
    )(where, *columns, *mine, other.reshape(4, 8, 16, 1024))


def body(integrals, occ_density, virt_density, screen):
    aux_rows, local_pairs, orbitals = integrals.shape
    blocks = screen.shape[0]
    grouped = integrals.reshape(blocks, aux_rows // blocks, local_pairs, orbitals)
    screened = jnp.where(screen[:, None, :, None] > 0, grouped, jnp.zeros_like(grouped)).reshape(
        aux_rows, local_pairs, orbitals
    )
    virtual = jnp.dot(
        screened.reshape(aux_rows * local_pairs, orbitals),
        virt_density,
        preferred_element_type=jnp.float32,
    ).astype(jnp.bfloat16).reshape(aux_rows, local_pairs, orbitals)
    got = lax.all_to_all(pack(jnp.stack([screened, virtual])), GROUP, 0, 0, tiled=True)
    own = unpack(got[:, :, :64])
    up = lax.ppermute(own, "y_hi", ring(1))
    down = lax.ppermute(own, "y_hi", ring(-1))
    core = lax.axis_index("core")
    far = lax.ppermute(jnp.where(core == 0, up, down), TALL, y_hop())
    spread = (jnp.arange(1024)[:, None] // 32 == jnp.arange(32)[None, :]).astype(jnp.bfloat16)
    tall = jnp.dot(spread, occ_density)
    full = lax.dot_general(tall, spread, (((1,), (1,)), ((), ())))
    same = jnp.arange(1024)[:, None] % 32 == jnp.arange(1024)[None, :] % 32
    mixer = jnp.where(same, full, jnp.zeros_like(full))
    occupied = jnp.dot(unpack(got[:, :, 64:]), mixer, preferred_element_type=jnp.float32)
    occupied = occupied.astype(jnp.bfloat16)
    near = lax.ppermute(occupied, WIDE, x_hop(True))
    back = lax.ppermute(occupied, WIDE, x_hop(False))
    beyond = lax.ppermute(near, WIDE, x_hop(True))
    mine = [occupied, near, beyond, back]
    other = lax.ppermute(jnp.stack(mine), "core", [(0, 1), (1, 0)])
    place = lax.axis_index("x_hi") * 2 + lax.axis_index("x_lo")
    where = jnp.stack([lax.axis_index("y_hi"), place, core]).astype(jnp.int32)
    tiles = multiply(where, [own, up, down, far], mine, other)
    got = lax.all_to_all(tiles, GROUP, 0, 0, tiled=True)
    total = jnp.sum(got.reshape(2, 2, 2, 8, 2, 2, 16, 128).astype(jnp.float32), axis=(1, 3))
    return total.transpose(5, 3, 0, 1, 2, 4).reshape(128, 256)


def solution(mesh):
    fine = Mesh(mesh.devices.reshape(2, 4, 2, 2, 8, 2), AUX + PAIR)
    placed = (P(AUX, PAIR, None), P(), P(), P(AUX, PAIR))

    return jax.shard_map(body, mesh=fine, in_specs=placed, out_specs=P(AUX, PAIR), check_vma=False)
```

```python
import jax
import jax.numpy as jnp
from jax import lax
from jax.experimental import pallas as pl
from jax.experimental.pallas import tpu as pltpu
from jax.sharding import Mesh, PartitionSpec as P


AUX = ("x_lo", "y", "core")
PAIR = ("z", "x_hi")
PLANE = ("x_lo", "core", "z", "x_hi")
WIDE = ("x_lo", "core", "x_hi")


def ring(step):
    return [(y, (y + step) % 8) for y in range(8)]


def y_hop(steps):
    return [(y * 2 + c, (y + steps * (1 - 2 * c)) % 8 * 2 + c) for y in range(8) for c in range(2)]


def wide_index(place, core):
    return place % 2 * 4 + core * 2 + place // 2


def x_hop(first):
    pairs = []
    for place in range(4):
        for core in range(2):
            step = 1 if (core == 0) == first else -1
            pairs.append((wide_index(place, core), wide_index((place + step) % 4, core)))
    return pairs


def pack(values):
    pieces = values.reshape(2, 2, 2, 16, 2, 8, 64)
    return pieces.transpose(0, 1, 5, 2, 3, 4, 6).reshape(64, 16, 128)


def unpack(got):
    return got.reshape(4, 16, 16, 128).transpose(0, 2, 1, 3).reshape(64, 2048)


def multiply_kernel(where_ref, *refs):
    columns, mine, other, (out_ref, left, right, done) = refs[:8], refs[8:12], refs[12], refs[13:]
    y, place, core = where_ref[0], where_ref[1], where_ref[2]
    copies = []

    def bring(source, target):
        copies.append(pltpu.make_async_copy(source, target, done.at[len(copies)]))
        copies[-1].start()

    for i, steps in enumerate((0, 1, 2, 3, -1, -2, -3, 4)):
        at = lax.rem(y - steps + 8, 8)
        bring(columns[i], left.at[pl.ds(pl.multiple_of(at * 64, 64), 64), :])
    sign = 1 - 2 * core
    for i, steps in enumerate((0, 1, 2, -1)):
        for near in range(2):
            step = sign * steps if near else -sign * steps
            source = lax.rem(place - step + 8, 4)
            owner = core if near else 1 - core
            at = lax.rem(source, 2) * 4 + owner * 2 + source // 2
            bring(mine[i] if near else other.at[i], right.at[:, pl.ds(pl.multiple_of(at * 16, 16), 16), :])
    for copy in copies:
        copy.wait()
    for part_id in range(2):
        part = lax.dot_general(
            left[part_id * 256 : part_id * 256 + 256, :],
            right[...].reshape(512, 2048),
            (((1,), (1,)), ((), ())),
            preferred_element_type=jnp.float32,
        ).astype(jnp.bfloat16)
        for y_column in range(4):
            for x_lo_q in range(2):
                for group in range(4):
                    row = y_column * 64 + x_lo_q * 32
                    dest = group * 16 + (x_lo_q * 4 + part_id * 2 + y_column // 2) * 2 + y_column % 2
                    out_ref[dest] = part[row : row + 32, group * 128 : group * 128 + 128]


def multiply(where, columns, mine, other):
    mine = [block.reshape(4, 16, 2048) for block in mine]
    return pl.pallas_call(
        multiply_kernel,
        out_shape=jax.ShapeDtypeStruct((64, 32, 128), jnp.bfloat16),
        in_specs=[pl.BlockSpec(memory_space=pltpu.SMEM)] + [pl.BlockSpec(memory_space=pl.ANY)] * 13,
        out_specs=pl.BlockSpec(memory_space=pltpu.VMEM),
        scratch_shapes=[
            pltpu.VMEM((512, 2048), jnp.bfloat16),
            pltpu.VMEM((4, 128, 2048), jnp.bfloat16),
            pltpu.SemaphoreType.DMA((16,)),
        ],
        compiler_params=pltpu.CompilerParams(vmem_limit_bytes=20 * 1024 * 1024),
        cost_estimate=pl.CostEstimate(flops=2 * 512 * 512 * 2048, bytes_accessed=4 << 20, transcendentals=0),
    )(where, *columns, *mine, other.reshape(4, 4, 16, 2048))


def body(integrals, occ_density, virt_density, screen):
    aux_rows, local_pairs, orbitals = integrals.shape
    blocks = screen.shape[0]
    grouped = integrals.reshape(blocks, aux_rows // blocks, local_pairs, orbitals)
    screened = jnp.where(screen[:, None, :, None] > 0, grouped, jnp.zeros_like(grouped)).reshape(
        aux_rows, local_pairs, orbitals
    )
    virtual = jnp.dot(
        screened.reshape(aux_rows * local_pairs, orbitals),
        virt_density,
        preferred_element_type=jnp.float32,
    ).astype(jnp.bfloat16).reshape(aux_rows, local_pairs, orbitals)
    both = jnp.concatenate([pack(screened), pack(virtual)], axis=1)
    got = lax.all_to_all(both, PLANE, 0, 0, tiled=True)
    own = unpack(got[:, :16])
    core = lax.axis_index("core")
    up1 = lax.ppermute(own, "y", ring(1))
    down1 = lax.ppermute(own, "y", ring(-1))
    up2 = lax.ppermute(own, "y", ring(2))
    down2 = lax.ppermute(own, "y", ring(-2))
    up3 = lax.ppermute(up2, "y", ring(1))
    down3 = lax.ppermute(down2, "y", ring(-1))
    far = lax.ppermute(jnp.where(core == 0, up2, down2), ("y", "core"), y_hop(2))
    columns = [own, up1, up2, up3, down1, down2, down3, far]
    virt_rows = unpack(got[:, 16:]).reshape(64, 32, 64)
    occupied = jnp.einsum("pms,ml->pls", virt_rows, occ_density, preferred_element_type=jnp.float32)
    occupied = lax.optimization_barrier(occupied.astype(jnp.bfloat16).reshape(64, 2048))
    near = lax.ppermute(occupied, WIDE, x_hop(True))
    back = lax.ppermute(occupied, WIDE, x_hop(False))
    far = lax.ppermute(near, WIDE, x_hop(True))
    mine = [occupied, near, far, back]
    other = lax.ppermute(jnp.stack(mine), "core", [(0, 1), (1, 0)])
    place = lax.axis_index("x_hi") * 2 + lax.axis_index("x_lo")
    where = jnp.stack([lax.axis_index("y"), place, core]).astype(jnp.int32)
    tiles = multiply(where, columns, mine, other)
    got = lax.all_to_all(tiles, PLANE, 0, 0, tiled=True)
    total = jnp.sum(got.reshape(2, 2, 8, 2, 2, 16, 128).astype(jnp.float32), axis=2)
    return total.transpose(5, 3, 0, 1, 2, 4).reshape(128, 256)


def solution(mesh):
    fine = Mesh(mesh.devices.reshape(2, 8, 2, 8, 2), AUX + PAIR)
    placed = (P(AUX, PAIR, None), P(), P(), P(AUX, PAIR))

    return jax.shard_map(body, mesh=fine, in_specs=placed, out_specs=P(AUX, PAIR), check_vma=False)
```

```python
import jax
import jax.numpy as jnp
from jax import lax
from jax.experimental import pallas as pl
from jax.experimental.pallas import tpu as pltpu
from jax.sharding import Mesh, PartitionSpec as P


AUX = ("x_lo", "y", "core")
PAIR = ("z", "x_hi")
PLANE = ("x_lo", "core", "z", "x_hi")
WIDE = ("x_lo", "core", "x_hi")


def ring(step):
    return [(y, (y + step) % 8) for y in range(8)]


def wide_index(place, core):
    return place % 2 * 4 + core * 2 + place // 2


def x_hop():
    return [
        (wide_index(place, core), wide_index((place + 1 - 2 * core) % 4, core))
        for place in range(4)
        for core in range(2)
    ]


def pack(values):
    pieces = values.reshape(2, 2, 2, 16, 2, 8, 64)
    return pieces.transpose(0, 1, 5, 2, 3, 4, 6).reshape(64, 16, 128)


def unpack(got):
    return got.reshape(4, 16, 16, 128).transpose(0, 2, 1, 3).reshape(64, 2048)


def multiply_kernel(where_ref, *refs):
    columns, mine, other, (out_ref, left, right, done) = refs[:8], refs[8:12], refs[12], refs[13:]
    y, place, core = where_ref[0], where_ref[1], where_ref[2]
    copies = []

    def bring(source, target):
        copies.append(pltpu.make_async_copy(source, target, done.at[len(copies)]))
        copies[-1].start()

    for i, steps in enumerate((0, 1, 2, 3, -1, -2, -3, 4)):
        at = lax.rem(y - steps + 8, 8)
        bring(columns[i], left.at[pl.ds(pl.multiple_of(at * 64, 64), 64), :])
    sign = 1 - 2 * core
    for i, steps in enumerate((0, 1, 2, 3)):
        for near in range(2):
            step = sign * steps if near else -sign * steps
            source = lax.rem(place - step + 8, 4)
            owner = core if near else 1 - core
            at = lax.rem(source, 2) * 4 + owner * 2 + source // 2
            bring(mine[i] if near else other.at[i], right.at[:, pl.ds(pl.multiple_of(at * 16, 16), 16), :])
    for copy in copies:
        copy.wait()
    for part_id in range(2):
        part = lax.dot_general(
            left[part_id * 256 : part_id * 256 + 256, :],
            right[...].reshape(512, 2048),
            (((1,), (1,)), ((), ())),
            preferred_element_type=jnp.float32,
        ).astype(jnp.bfloat16)
        for y_column in range(4):
            for x_lo_q in range(2):
                for group in range(4):
                    row = y_column * 64 + x_lo_q * 32
                    dest = group * 16 + (x_lo_q * 4 + part_id * 2 + y_column // 2) * 2 + y_column % 2
                    out_ref[dest] = part[row : row + 32, group * 128 : group * 128 + 128]


def multiply(where, columns, mine, other):
    mine = [block.reshape(4, 16, 2048) for block in mine]
    return pl.pallas_call(
        multiply_kernel,
        out_shape=jax.ShapeDtypeStruct((64, 32, 128), jnp.bfloat16),
        in_specs=[pl.BlockSpec(memory_space=pltpu.SMEM)] + [pl.BlockSpec(memory_space=pl.ANY)] * 13,
        out_specs=pl.BlockSpec(memory_space=pltpu.VMEM),
        scratch_shapes=[
            pltpu.VMEM((512, 2048), jnp.bfloat16),
            pltpu.VMEM((4, 128, 2048), jnp.bfloat16),
            pltpu.SemaphoreType.DMA((16,)),
        ],
        compiler_params=pltpu.CompilerParams(vmem_limit_bytes=20 * 1024 * 1024),
        cost_estimate=pl.CostEstimate(flops=2 * 512 * 512 * 2048, bytes_accessed=4 << 20, transcendentals=0),
    )(where, *columns, *mine, other.reshape(4, 4, 16, 2048))


def body(integrals, occ_density, virt_density, screen):
    aux_rows, local_pairs, orbitals = integrals.shape
    blocks = screen.shape[0]
    grouped = integrals.reshape(blocks, aux_rows // blocks, local_pairs, orbitals)
    screened = jnp.where(screen[:, None, :, None] > 0, grouped, jnp.zeros_like(grouped)).reshape(
        aux_rows, local_pairs, orbitals
    )
    virtual = jnp.dot(
        screened.reshape(aux_rows * local_pairs, orbitals),
        virt_density,
        preferred_element_type=jnp.float32,
    ).astype(jnp.bfloat16).reshape(aux_rows, local_pairs, orbitals)
    both = jnp.concatenate([pack(screened), pack(virtual)], axis=1)
    got = lax.all_to_all(both, PLANE, 0, 0, tiled=True)
    own = unpack(got[:, :16])
    core = lax.axis_index("core")
    up1 = lax.ppermute(own, "y", ring(1))
    down1 = lax.ppermute(own, "y", ring(-1))
    up2 = lax.ppermute(own, "y", ring(2))
    down2 = lax.ppermute(own, "y", ring(-2))
    up3 = lax.ppermute(up2, "y", ring(1))
    down3 = lax.ppermute(down2, "y", ring(-1))
    far = lax.ppermute(up2, "y", ring(2))
    columns = [own, up1, up2, up3, down1, down2, down3, far]
    virt_rows = unpack(got[:, 16:]).reshape(64, 32, 64)
    occupied = jnp.einsum("pms,ml->pls", virt_rows, occ_density, preferred_element_type=jnp.float32)
    occupied = lax.optimization_barrier(occupied.astype(jnp.bfloat16).reshape(64, 2048))
    mine = [occupied]
    for _ in range(3):
        mine.append(lax.ppermute(mine[-1], WIDE, x_hop()))
    other = lax.ppermute(jnp.stack(mine), "core", [(0, 1), (1, 0)])
    place = lax.axis_index("x_hi") * 2 + lax.axis_index("x_lo")
    where = jnp.stack([lax.axis_index("y"), place, core]).astype(jnp.int32)
    tiles = multiply(where, columns, mine, other)
    got = lax.all_to_all(tiles, PLANE, 0, 0, tiled=True)
    total = jnp.sum(got.reshape(2, 2, 8, 2, 2, 16, 128).astype(jnp.float32), axis=2)
    return total.transpose(5, 3, 0, 1, 2, 4).reshape(128, 256)


def solution(mesh):
    fine = Mesh(mesh.devices.reshape(2, 8, 2, 8, 2), AUX + PAIR)
    placed = (P(AUX, PAIR, None), P(), P(), P(AUX, PAIR))

    return jax.shard_map(body, mesh=fine, in_specs=placed, out_specs=P(AUX, PAIR), check_vma=False)
```

```python
import jax
import jax.numpy as jnp
from jax import lax
from jax.experimental import pallas as pl
from jax.experimental.pallas import tpu as pltpu
from jax.sharding import Mesh, PartitionSpec as P


AUX = ("x_lo", "y", "core")
PAIR = ("z", "x_hi")
PLANE = ("x_lo", "core", "z", "x_hi")
WIDE = ("x_lo", "core", "x_hi")


def ring(step):
    return [(y, (y + step) % 8) for y in range(8)]


def wide_index(place, core):
    return place % 2 * 4 + core * 2 + place // 2


def x_hop():
    return [
        (wide_index(place, core), wide_index((place + 1 - 2 * core) % 4, core))
        for place in range(4)
        for core in range(2)
    ]


def prepare_kernel(screen_ref, values_ref, density_ref, out_ref, kept, virtual):
    row = lax.broadcasted_iota(jnp.int32, (256, 512), 0)
    first = jnp.where(row % 2 == 0, screen_ref[0, 0], screen_ref[0, 1])
    second = jnp.where(row % 2 == 0, screen_ref[1, 0], screen_ref[1, 1])
    keep = jnp.where(row < 128, first, second) > 0
    screened = jnp.where(keep, values_ref[...].astype(jnp.float32), 0.0)
    product = jnp.dot(screened.astype(jnp.bfloat16), density_ref[...], preferred_element_type=jnp.float32)
    for tile in range(4):
        kept[tile] = screened[:, tile * 128 : tile * 128 + 128]
        virtual[tile] = product[:, tile * 128 : tile * 128 + 128]
    for which, source in enumerate((kept, virtual)):
        for tile in range(4):
            even = source[tile, pl.ds(0, 128, stride=2), :]
            odd = source[tile, pl.ds(1, 128, stride=2), :]
            for half in range(2):
                cut = slice(half * 64, half * 64 + 64)
                block = jnp.concatenate([even[:, cut], odd[:, cut]], axis=1).astype(jnp.bfloat16)
                for w in range(8):
                    dest = w // 2 * 16 + (tile * 2 + half) * 2 + w % 2
                    out_ref[dest, which * 16 : which * 16 + 16, :] = block[w * 16 : w * 16 + 16, :]


def prepare(screen, integrals, virt_density):
    vmem = pl.BlockSpec(memory_space=pltpu.VMEM)
    return pl.pallas_call(
        prepare_kernel,
        out_shape=jax.ShapeDtypeStruct((64, 32, 128), jnp.bfloat16),
        in_specs=[pl.BlockSpec(memory_space=pltpu.SMEM), vmem, vmem],
        out_specs=vmem,
        scratch_shapes=[pltpu.VMEM((4, 256, 128), jnp.float32), pltpu.VMEM((4, 256, 128), jnp.float32)],
        compiler_params=pltpu.CompilerParams(vmem_limit_bytes=8 * 1024 * 1024),
    )(screen, integrals.reshape(256, 512), virt_density)


def unpack(got):
    return got.reshape(4, 16, 16, 128).transpose(0, 2, 1, 3).reshape(64, 2048)


def multiply_kernel(where_ref, *refs):
    columns, mine, other, (out_ref, left, right, done) = refs[:8], refs[8:12], refs[12], refs[13:]
    y, place, core = where_ref[0], where_ref[1], where_ref[2]
    copies = []

    def bring(source, target):
        copies.append(pltpu.make_async_copy(source, target, done.at[len(copies)]))
        copies[-1].start()

    for i, steps in enumerate((0, 1, 2, 3, -1, -2, -3, 4)):
        at = lax.rem(y - steps + 8, 8)
        bring(columns[i], left.at[pl.ds(pl.multiple_of(at * 64, 64), 64), :])
    sign = 1 - 2 * core
    for i, steps in enumerate((0, 1, 2, 3)):
        for near in range(2):
            step = sign * steps if near else -sign * steps
            source = lax.rem(place - step + 8, 4)
            owner = core if near else 1 - core
            at = lax.rem(source, 2) * 4 + owner * 2 + source // 2
            bring(mine[i] if near else other.at[i], right.at[:, pl.ds(pl.multiple_of(at * 16, 16), 16), :])
    for copy in copies:
        copy.wait()
    for part_id in range(2):
        part = lax.dot_general(
            left[part_id * 256 : part_id * 256 + 256, :],
            right[...].reshape(512, 2048),
            (((1,), (1,)), ((), ())),
            preferred_element_type=jnp.float32,
        ).astype(jnp.bfloat16)
        for y_column in range(4):
            for x_lo_q in range(2):
                for group in range(4):
                    row = y_column * 64 + x_lo_q * 32
                    dest = group * 16 + (x_lo_q * 4 + part_id * 2 + y_column // 2) * 2 + y_column % 2
                    out_ref[dest] = part[row : row + 32, group * 128 : group * 128 + 128]


def multiply(where, columns, mine, other):
    mine = [block.reshape(4, 16, 2048) for block in mine]
    return pl.pallas_call(
        multiply_kernel,
        out_shape=jax.ShapeDtypeStruct((64, 32, 128), jnp.bfloat16),
        in_specs=[pl.BlockSpec(memory_space=pltpu.SMEM)] + [pl.BlockSpec(memory_space=pl.ANY)] * 13,
        out_specs=pl.BlockSpec(memory_space=pltpu.VMEM),
        scratch_shapes=[
            pltpu.VMEM((512, 2048), jnp.bfloat16),
            pltpu.VMEM((4, 128, 2048), jnp.bfloat16),
            pltpu.SemaphoreType.DMA((16,)),
        ],
        compiler_params=pltpu.CompilerParams(vmem_limit_bytes=20 * 1024 * 1024),
        cost_estimate=pl.CostEstimate(flops=2 * 512 * 512 * 2048, bytes_accessed=4 << 20, transcendentals=0),
    )(where, *columns, *mine, other.reshape(4, 4, 16, 2048))


def body(integrals, occ_density, virt_density, screen):
    got = lax.all_to_all(prepare(screen, integrals, virt_density), PLANE, 0, 0, tiled=True)
    own = unpack(got[:, :16])
    core = lax.axis_index("core")
    up1 = lax.ppermute(own, "y", ring(1))
    down1 = lax.ppermute(own, "y", ring(-1))
    up2 = lax.ppermute(own, "y", ring(2))
    down2 = lax.ppermute(own, "y", ring(-2))
    up3 = lax.ppermute(up2, "y", ring(1))
    down3 = lax.ppermute(down2, "y", ring(-1))
    far = lax.ppermute(up3, "y", ring(1))
    columns = [own, up1, up2, up3, down1, down2, down3, far]
    virt_rows = unpack(got[:, 16:]).reshape(64, 32, 64)
    occupied = jnp.einsum("pms,ml->pls", virt_rows, occ_density, preferred_element_type=jnp.float32)
    occupied = lax.optimization_barrier(occupied.astype(jnp.bfloat16).reshape(64, 2048))
    mine = [occupied]
    for _ in range(3):
        mine.append(lax.ppermute(mine[-1], WIDE, x_hop()))
    other = lax.ppermute(jnp.stack(mine), "core", [(0, 1), (1, 0)])
    place = lax.axis_index("x_hi") * 2 + lax.axis_index("x_lo")
    where = jnp.stack([lax.axis_index("y"), place, core]).astype(jnp.int32)
    tiles = multiply(where, columns, mine, other)
    got = lax.all_to_all(tiles, PLANE, 0, 0, tiled=True)
    total = jnp.sum(got.reshape(2, 2, 8, 2, 2, 16, 128).astype(jnp.float32), axis=2)
    return total.transpose(5, 3, 0, 1, 2, 4).reshape(128, 256)


def solution(mesh):
    fine = Mesh(mesh.devices.reshape(2, 8, 2, 8, 2), AUX + PAIR)
    placed = (P(AUX, PAIR, None), P(), P(), P(AUX, PAIR))

    return jax.shard_map(body, mesh=fine, in_specs=placed, out_specs=P(AUX, PAIR), check_vma=False)
```

```python
import jax
import jax.numpy as jnp
from jax import lax
from jax.experimental import pallas as pl
from jax.experimental.pallas import tpu as pltpu
from jax.sharding import Mesh, PartitionSpec as P


AUX = ("x_lo", "y", "core")
PAIR = ("z", "x_hi")
PLANE = ("x_lo", "core", "z", "x_hi")
XX = ("x_lo", "x_hi")


def ring(step):
    return [(y, (y + step) % 8) for y in range(8)]


def prepare_kernel(screen_ref, values_ref, density_ref, out_ref, kept, virtual):
    row = lax.broadcasted_iota(jnp.int32, (256, 512), 0)
    first = jnp.where(row % 2 == 0, screen_ref[0, 0], screen_ref[0, 1])
    second = jnp.where(row % 2 == 0, screen_ref[1, 0], screen_ref[1, 1])
    keep = jnp.where(row < 128, first, second) > 0
    screened = jnp.where(keep, values_ref[...].astype(jnp.float32), 0.0)
    product = jnp.dot(screened.astype(jnp.bfloat16), density_ref[...], preferred_element_type=jnp.float32)
    for tile in range(4):
        kept[tile] = screened[:, tile * 128 : tile * 128 + 128]
        virtual[tile] = product[:, tile * 128 : tile * 128 + 128]
    for which, source in enumerate((kept, virtual)):
        for tile in range(4):
            even = source[tile, pl.ds(0, 128, stride=2), :]
            odd = source[tile, pl.ds(1, 128, stride=2), :]
            for half in range(2):
                cut = slice(half * 64, half * 64 + 64)
                block = jnp.concatenate([even[:, cut], odd[:, cut]], axis=1).astype(jnp.bfloat16)
                for w in range(8):
                    dest = w // 2 * 16 + (tile * 2 + half) * 2 + w % 2
                    out_ref[dest, which * 16 : which * 16 + 16, :] = block[w * 16 : w * 16 + 16, :]


def prepare(screen, integrals, virt_density):
    vmem = pl.BlockSpec(memory_space=pltpu.VMEM)
    return pl.pallas_call(
        prepare_kernel,
        out_shape=jax.ShapeDtypeStruct((64, 32, 128), jnp.bfloat16),
        in_specs=[pl.BlockSpec(memory_space=pltpu.SMEM), vmem, vmem],
        out_specs=vmem,
        scratch_shapes=[pltpu.VMEM((4, 256, 128), jnp.float32), pltpu.VMEM((4, 256, 128), jnp.float32)],
        compiler_params=pltpu.CompilerParams(vmem_limit_bytes=8 * 1024 * 1024),
    )(screen, integrals.reshape(256, 512), virt_density)


def unpack(got):
    return got.reshape(4, 16, 16, 128).transpose(0, 2, 1, 3).reshape(64, 2048)


def multiply_kernel(where_ref, *refs):
    columns, mine, other, (out_ref, left, right, done) = refs[:8], refs[8], refs[9], refs[10:]
    y, core = where_ref[0], where_ref[1]
    copies = []

    def bring(source, target):
        copies.append(pltpu.make_async_copy(source, target, done.at[len(copies)]))
        copies[-1].start()

    for i, steps in enumerate((0, 1, 2, 3, -1, -2, -3, 4)):
        at = lax.rem(y - steps + 8, 8)
        bring(columns[i], left.at[pl.ds(pl.multiple_of(at * 64, 64), 64), :])
    for i in range(4):
        for blocks, owner in ((mine, core), (other, 1 - core)):
            at = i // 2 * 4 + owner * 2 + i % 2
            bring(blocks.at[i], right.at[:, pl.ds(pl.multiple_of(at * 16, 16), 16), :])
    for copy in copies:
        copy.wait()
    for part_id in range(2):
        part = lax.dot_general(
            left[part_id * 256 : part_id * 256 + 256, :],
            right[...].reshape(512, 2048),
            (((1,), (1,)), ((), ())),
            preferred_element_type=jnp.float32,
        ).astype(jnp.bfloat16)
        for y_column in range(4):
            for x_lo_q in range(2):
                for group in range(4):
                    row = y_column * 64 + x_lo_q * 32
                    dest = group * 16 + (x_lo_q * 4 + part_id * 2 + y_column // 2) * 2 + y_column % 2
                    out_ref[dest] = part[row : row + 32, group * 128 : group * 128 + 128]


def multiply(where, columns, mine, other):
    return pl.pallas_call(
        multiply_kernel,
        out_shape=jax.ShapeDtypeStruct((64, 32, 128), jnp.bfloat16),
        in_specs=[pl.BlockSpec(memory_space=pltpu.SMEM)] + [pl.BlockSpec(memory_space=pl.ANY)] * 10,
        out_specs=pl.BlockSpec(memory_space=pltpu.VMEM),
        scratch_shapes=[
            pltpu.VMEM((512, 2048), jnp.bfloat16),
            pltpu.VMEM((4, 128, 2048), jnp.bfloat16),
            pltpu.SemaphoreType.DMA((16,)),
        ],
        compiler_params=pltpu.CompilerParams(vmem_limit_bytes=20 * 1024 * 1024),
        cost_estimate=pl.CostEstimate(flops=2 * 512 * 512 * 2048, bytes_accessed=4 << 20, transcendentals=0),
    )(where, *columns, mine.reshape(4, 4, 16, 2048), other.reshape(4, 4, 16, 2048))


def body(integrals, occ_density, virt_density, screen):
    got = lax.all_to_all(prepare(screen, integrals, virt_density), PLANE, 0, 0, tiled=True)
    own = unpack(got[:, :16])
    core = lax.axis_index("core")
    up1 = lax.ppermute(own, "y", ring(1))
    down1 = lax.ppermute(own, "y", ring(-1))
    up2 = lax.ppermute(own, "y", ring(2))
    down2 = lax.ppermute(own, "y", ring(-2))
    up3 = lax.ppermute(up2, "y", ring(1))
    down3 = lax.ppermute(down2, "y", ring(-1))
    far = lax.ppermute(up3, "y", ring(1))
    columns = [own, up1, up2, up3, down1, down2, down3, far]
    virt_rows = unpack(got[:, 16:]).reshape(64, 32, 64)
    occupied = jnp.einsum("pms,ml->pls", virt_rows, occ_density, preferred_element_type=jnp.float32)
    occupied = lax.optimization_barrier(occupied.astype(jnp.bfloat16).reshape(64, 2048))
    mine = lax.all_to_all(jnp.broadcast_to(occupied, (4, 64, 2048)), XX, 0, 0, tiled=True)
    other = lax.ppermute(mine, "core", [(0, 1), (1, 0)])
    where = jnp.stack([lax.axis_index("y"), core]).astype(jnp.int32)
    tiles = multiply(where, columns, mine, other)
    got = lax.all_to_all(tiles, PLANE, 0, 0, tiled=True)
    total = jnp.sum(got.reshape(2, 2, 8, 2, 2, 16, 128).astype(jnp.float32), axis=2)
    return total.transpose(5, 3, 0, 1, 2, 4).reshape(128, 256)


def solution(mesh):
    fine = Mesh(mesh.devices.reshape(2, 8, 2, 8, 2), AUX + PAIR)
    placed = (P(AUX, PAIR, None), P(), P(), P(AUX, PAIR))

    return jax.shard_map(body, mesh=fine, in_specs=placed, out_specs=P(AUX, PAIR), check_vma=False)
```

```python
import jax
import jax.numpy as jnp
from jax import lax
from jax.experimental import pallas as pl
from jax.experimental.pallas import tpu as pltpu
from jax.sharding import Mesh, PartitionSpec as P


AUX = ("x_lo", "y", "core")
PAIR = ("z", "x_hi")
PLANE = ("x_lo", "core", "z", "x_hi")
XX = ("x_lo", "x_hi")


def ring(step):
    return [(y, (y + step) % 8) for y in range(8)]


def prepare_kernel(screen_ref, values_ref, density_ref, out_ref, kept, virtual):
    row = lax.broadcasted_iota(jnp.int32, (256, 512), 0)
    first = jnp.where(row % 2 == 0, screen_ref[0, 0], screen_ref[0, 1])
    second = jnp.where(row % 2 == 0, screen_ref[1, 0], screen_ref[1, 1])
    keep = jnp.where(row < 128, first, second) > 0
    screened = jnp.where(keep, values_ref[...].astype(jnp.float32), 0.0)
    product = jnp.dot(screened.astype(jnp.bfloat16), density_ref[...], preferred_element_type=jnp.float32)
    for tile in range(4):
        kept[tile] = screened[:, tile * 128 : tile * 128 + 128]
        virtual[tile] = product[:, tile * 128 : tile * 128 + 128]
    for which, source in enumerate((kept, virtual)):
        for tile in range(4):
            even = source[tile, pl.ds(0, 128, stride=2), :]
            odd = source[tile, pl.ds(1, 128, stride=2), :]
            for half in range(2):
                cut = slice(half * 64, half * 64 + 64)
                block = jnp.concatenate([even[:, cut], odd[:, cut]], axis=1).astype(jnp.bfloat16)
                for w in range(8):
                    dest = w // 2 * 16 + (tile * 2 + half) * 2 + w % 2
                    out_ref[dest, which * 16 : which * 16 + 16, :] = block[w * 16 : w * 16 + 16, :]


def prepare(screen, integrals, virt_density):
    vmem = pl.BlockSpec(memory_space=pltpu.VMEM)
    return pl.pallas_call(
        prepare_kernel,
        out_shape=jax.ShapeDtypeStruct((64, 32, 128), jnp.bfloat16),
        in_specs=[pl.BlockSpec(memory_space=pltpu.SMEM), vmem, vmem],
        out_specs=vmem,
        scratch_shapes=[pltpu.VMEM((4, 256, 128), jnp.float32), pltpu.VMEM((4, 256, 128), jnp.float32)],
        compiler_params=pltpu.CompilerParams(vmem_limit_bytes=8 * 1024 * 1024),
    )(screen, integrals.reshape(256, 512), virt_density)


def unpack(got):
    return got.reshape(4, 16, 16, 128).transpose(0, 2, 1, 3).reshape(64, 2048)


def multiply_kernel(where_ref, *refs):
    columns, mine, other, (out_ref, left, right, done) = refs[:8], refs[8], refs[9], refs[10:]
    y, core = where_ref[0], where_ref[1]
    copies = []

    def bring(source, target):
        copies.append(pltpu.make_async_copy(source, target, done.at[len(copies)]))
        copies[-1].start()

    for i, steps in enumerate((0, 1, 2, 3, -1, -2, -3, 4)):
        at = lax.rem(y - steps + 8, 8)
        bring(columns[i], left.at[pl.ds(pl.multiple_of(at * 64, 64), 64), :])
    for i in range(4):
        for blocks, owner in ((mine, core), (other, 1 - core)):
            at = i // 2 * 4 + owner * 2 + i % 2
            bring(blocks.at[i], right.at[:, pl.ds(pl.multiple_of(at * 16, 16), 16), :])
    for copy in copies:
        copy.wait()
    for part_id in range(2):
        part = lax.dot_general(
            left[part_id * 256 : part_id * 256 + 256, :],
            right[...].reshape(512, 2048),
            (((1,), (1,)), ((), ())),
            preferred_element_type=jnp.float32,
        ).astype(jnp.bfloat16)
        for y_column in range(4):
            for x_lo_q in range(2):
                for group in range(4):
                    row = y_column * 64 + x_lo_q * 32
                    dest = group * 16 + (x_lo_q * 4 + part_id * 2 + y_column // 2) * 2 + y_column % 2
                    out_ref[dest] = part[row : row + 32, group * 128 : group * 128 + 128]


def multiply(where, columns, mine, other):
    return pl.pallas_call(
        multiply_kernel,
        out_shape=jax.ShapeDtypeStruct((64, 32, 128), jnp.bfloat16),
        in_specs=[pl.BlockSpec(memory_space=pltpu.SMEM)] + [pl.BlockSpec(memory_space=pl.ANY)] * 10,
        out_specs=pl.BlockSpec(memory_space=pltpu.VMEM),
        scratch_shapes=[
            pltpu.VMEM((512, 2048), jnp.bfloat16),
            pltpu.VMEM((4, 128, 2048), jnp.bfloat16),
            pltpu.SemaphoreType.DMA((16,)),
        ],
        compiler_params=pltpu.CompilerParams(vmem_limit_bytes=20 * 1024 * 1024),
        cost_estimate=pl.CostEstimate(flops=2 * 512 * 512 * 2048, bytes_accessed=4 << 20, transcendentals=0),
    )(where, *columns, mine.reshape(4, 4, 16, 2048), other.reshape(4, 4, 16, 2048))


def finish_kernel(tiles_ref, out_ref):
    for core_q in range(2):
        rows = pl.ds(core_q * 16, 16)
        parts = []
        for w in range(8):
            total = None
            for z in range(8):
                part = tiles_ref[w // 2 * 16 + z * 2 + w % 2, rows, :].astype(jnp.float32)
                total = part if total is None else total + part
            parts.append(total)
        out_ref[:, core_q * 128 : core_q * 128 + 128] = jnp.concatenate(parts, axis=0).T


def finish(tiles):
    vmem = pl.BlockSpec(memory_space=pltpu.VMEM)
    return pl.pallas_call(
        finish_kernel,
        out_shape=jax.ShapeDtypeStruct((128, 256), jnp.float32),
        in_specs=[vmem],
        out_specs=vmem,
        compiler_params=pltpu.CompilerParams(vmem_limit_bytes=8 * 1024 * 1024),
    )(tiles)


def body(integrals, occ_density, virt_density, screen):
    got = lax.all_to_all(prepare(screen, integrals, virt_density), PLANE, 0, 0, tiled=True)
    own = unpack(got[:, :16])
    core = lax.axis_index("core")
    up1 = lax.ppermute(own, "y", ring(1))
    down1 = lax.ppermute(own, "y", ring(-1))
    up2 = lax.ppermute(own, "y", ring(2))
    down2 = lax.ppermute(own, "y", ring(-2))
    up3 = lax.ppermute(up2, "y", ring(1))
    down3 = lax.ppermute(down2, "y", ring(-1))
    far = lax.ppermute(up3, "y", ring(1))
    columns = [own, up1, up2, up3, down1, down2, down3, far]
    virt_rows = unpack(got[:, 16:]).reshape(64, 32, 64)
    occupied = jnp.einsum("pms,ml->pls", virt_rows, occ_density, preferred_element_type=jnp.float32)
    occupied = lax.optimization_barrier(occupied.astype(jnp.bfloat16).reshape(64, 2048))
    mine = lax.all_to_all(jnp.broadcast_to(occupied, (4, 64, 2048)), XX, 0, 0, tiled=True)
    other = lax.ppermute(mine, "core", [(0, 1), (1, 0)])
    where = jnp.stack([lax.axis_index("y"), core]).astype(jnp.int32)
    tiles = multiply(where, columns, mine, other)
    got = lax.all_to_all(tiles, PLANE, 0, 0, tiled=True)
    return finish(got)


def solution(mesh):
    fine = Mesh(mesh.devices.reshape(2, 8, 2, 8, 2), AUX + PAIR)
    placed = (P(AUX, PAIR, None), P(), P(), P(AUX, PAIR))

    return jax.shard_map(body, mesh=fine, in_specs=placed, out_specs=P(AUX, PAIR), check_vma=False)
```

```python
import jax
import jax.numpy as jnp
from jax import lax
from jax.experimental import pallas as pl
from jax.experimental.pallas import tpu as pltpu
from jax.sharding import Mesh, PartitionSpec as P


AUX = ("x_lo", "y", "core")
PAIR = ("z", "x_hi")
PLANE = ("x_lo", "core", "z", "x_hi")
XX = ("x_lo", "x_hi")


def ring(step):
    return [(y * 2 + c, (y + step * (1 - 2 * c)) % 8 * 2 + c) for y in range(8) for c in range(2)]


def prepare_kernel(screen_ref, values_ref, density_ref, out_ref, kept, virtual):
    row = lax.broadcasted_iota(jnp.int32, (256, 512), 0)
    first = jnp.where(row % 2 == 0, screen_ref[0, 0], screen_ref[0, 1])
    second = jnp.where(row % 2 == 0, screen_ref[1, 0], screen_ref[1, 1])
    keep = jnp.where(row < 128, first, second) > 0
    screened = jnp.where(keep, values_ref[...].astype(jnp.float32), 0.0)
    product = jnp.dot(screened.astype(jnp.bfloat16), density_ref[...], preferred_element_type=jnp.float32)
    for tile in range(4):
        kept[tile] = screened[:, tile * 128 : tile * 128 + 128]
        virtual[tile] = product[:, tile * 128 : tile * 128 + 128]
    for which, source in enumerate((kept, virtual)):
        for tile in range(4):
            even = source[tile, pl.ds(0, 128, stride=2), :]
            odd = source[tile, pl.ds(1, 128, stride=2), :]
            for half in range(2):
                cut = slice(half * 64, half * 64 + 64)
                block = jnp.concatenate([even[:, cut], odd[:, cut]], axis=1).astype(jnp.bfloat16)
                for w in range(8):
                    dest = w // 2 * 16 + (tile * 2 + half) * 2 + w % 2
                    out_ref[dest, which * 16 : which * 16 + 16, :] = block[w * 16 : w * 16 + 16, :]


def prepare(screen, integrals, virt_density):
    vmem = pl.BlockSpec(memory_space=pltpu.VMEM)
    return pl.pallas_call(
        prepare_kernel,
        out_shape=jax.ShapeDtypeStruct((64, 32, 128), jnp.bfloat16),
        in_specs=[pl.BlockSpec(memory_space=pltpu.SMEM), vmem, vmem],
        out_specs=vmem,
        scratch_shapes=[pltpu.VMEM((4, 256, 128), jnp.float32), pltpu.VMEM((4, 256, 128), jnp.float32)],
        compiler_params=pltpu.CompilerParams(vmem_limit_bytes=8 * 1024 * 1024),
    )(screen, integrals.reshape(256, 512), virt_density)


def unpack(got):
    return got.reshape(4, 16, 16, 128).transpose(0, 2, 1, 3).reshape(64, 2048)


def multiply_kernel(where_ref, *refs):
    columns, mine, other, (out_ref, left, right, done) = refs[:8], refs[8], refs[9], refs[10:]
    y, core = where_ref[0], where_ref[1]
    copies = []

    def bring(source, target):
        copies.append(pltpu.make_async_copy(source, target, done.at[len(copies)]))
        copies[-1].start()

    sign = 1 - 2 * core
    for i, steps in enumerate((0, 1, 2, 3, -1, -2, -3, 4)):
        at = lax.rem(y - sign * steps + 8, 8)
        bring(columns[i], left.at[pl.ds(pl.multiple_of(at * 64, 64), 64), :])
    for i in range(4):
        for blocks, owner in ((mine, core), (other, 1 - core)):
            at = i // 2 * 4 + owner * 2 + i % 2
            right[:, pl.ds(pl.multiple_of(at * 16, 16), 16), :] = blocks[i]
    for copy in copies:
        copy.wait()
    for part_id in range(2):
        part = lax.dot_general(
            left[part_id * 256 : part_id * 256 + 256, :],
            right[...].reshape(512, 2048),
            (((1,), (1,)), ((), ())),
            preferred_element_type=jnp.float32,
        ).astype(jnp.bfloat16)
        for y_column in range(4):
            for x_lo_q in range(2):
                for group in range(4):
                    row = y_column * 64 + x_lo_q * 32
                    dest = group * 16 + (x_lo_q * 4 + part_id * 2 + y_column // 2) * 2 + y_column % 2
                    out_ref[dest] = part[row : row + 32, group * 128 : group * 128 + 128]


def multiply(where, columns, mine, other):
    return pl.pallas_call(
        multiply_kernel,
        out_shape=jax.ShapeDtypeStruct((64, 32, 128), jnp.bfloat16),
        in_specs=[pl.BlockSpec(memory_space=pltpu.SMEM)]
        + [pl.BlockSpec(memory_space=pl.ANY)] * 8
        + [pl.BlockSpec(memory_space=pltpu.VMEM)] * 2,
        out_specs=pl.BlockSpec(memory_space=pltpu.VMEM),
        scratch_shapes=[
            pltpu.VMEM((512, 2048), jnp.bfloat16),
            pltpu.VMEM((4, 128, 2048), jnp.bfloat16),
            pltpu.SemaphoreType.DMA((8,)),
        ],
        compiler_params=pltpu.CompilerParams(vmem_limit_bytes=20 * 1024 * 1024),
        cost_estimate=pl.CostEstimate(flops=2 * 512 * 512 * 2048, bytes_accessed=4 << 20, transcendentals=0),
    )(where, *columns, mine.reshape(4, 4, 16, 2048), other.reshape(4, 4, 16, 2048))


def finish_kernel(tiles_ref, out_ref):
    for core_q in range(2):
        rows = pl.ds(core_q * 16, 16)
        parts = []
        for w in range(8):
            total = None
            for z in range(8):
                part = tiles_ref[w // 2 * 16 + z * 2 + w % 2, rows, :].astype(jnp.float32)
                total = part if total is None else total + part
            parts.append(total)
        out_ref[:, core_q * 128 : core_q * 128 + 128] = jnp.concatenate(parts, axis=0).T


def finish(tiles):
    vmem = pl.BlockSpec(memory_space=pltpu.VMEM)
    return pl.pallas_call(
        finish_kernel,
        out_shape=jax.ShapeDtypeStruct((128, 256), jnp.float32),
        in_specs=[vmem],
        out_specs=vmem,
        compiler_params=pltpu.CompilerParams(vmem_limit_bytes=8 * 1024 * 1024),
    )(tiles)


def body(integrals, occ_density, virt_density, screen):
    got = lax.all_to_all(prepare(screen, integrals, virt_density), PLANE, 0, 0, tiled=True)
    own = unpack(got[:, :16])
    core = lax.axis_index("core")
    up1 = lax.ppermute(own, ("y", "core"), ring(1))
    down1 = lax.ppermute(own, ("y", "core"), ring(-1))
    up2 = lax.ppermute(own, ("y", "core"), ring(2))
    down2 = lax.ppermute(own, ("y", "core"), ring(-2))
    up3 = lax.ppermute(up2, ("y", "core"), ring(1))
    down3 = lax.ppermute(down2, ("y", "core"), ring(-1))
    far = lax.ppermute(up2, ("y", "core"), ring(2))
    columns = [own, up1, up2, up3, down1, down2, down3, far]
    virt_rows = unpack(got[:, 16:]).reshape(64, 32, 64)
    occupied = jnp.einsum("pms,ml->pls", virt_rows, occ_density, preferred_element_type=jnp.float32)
    occupied = lax.optimization_barrier(occupied.astype(jnp.bfloat16).reshape(64, 2048))
    mine = lax.all_to_all(jnp.broadcast_to(occupied, (4, 64, 2048)), XX, 0, 0, tiled=True)
    other = lax.ppermute(mine, "core", [(0, 1), (1, 0)])
    where = jnp.stack([lax.axis_index("y"), core]).astype(jnp.int32)
    tiles = multiply(where, columns, mine, other)
    got = lax.all_to_all(tiles, PLANE, 0, 0, tiled=True)
    return finish(got)


def solution(mesh):
    fine = Mesh(mesh.devices.reshape(2, 8, 2, 8, 2), AUX + PAIR)
    placed = (P(AUX, PAIR, None), P(), P(), P(AUX, PAIR))

    return jax.shard_map(body, mesh=fine, in_specs=placed, out_specs=P(AUX, PAIR), check_vma=False)
```

```python
import jax
import jax.numpy as jnp
from jax import lax
from jax.experimental import pallas as pl
from jax.experimental.pallas import tpu as pltpu
from jax.sharding import Mesh, PartitionSpec as P


AUX = ("x_lo", "y", "core")
PAIR = ("z", "x_hi")
PLANE = ("x_lo", "core", "z", "x_hi")
XX = ("x_lo", "x_hi")


def ring(step):
    return [(y * 2 + c, (y + step * (1 - 2 * c)) % 8 * 2 + c) for y in range(8) for c in range(2)]


def prepare_kernel(screen_ref, values_ref, density_ref, out_ref, kept, virtual):
    row = lax.broadcasted_iota(jnp.int32, (256, 512), 0)
    first = jnp.where(row % 2 == 0, screen_ref[0, 0], screen_ref[0, 1])
    second = jnp.where(row % 2 == 0, screen_ref[1, 0], screen_ref[1, 1])
    keep = jnp.where(row < 128, first, second) > 0
    screened = jnp.where(keep, values_ref[...].astype(jnp.float32), 0.0)
    product = jnp.dot(screened.astype(jnp.bfloat16), density_ref[...], preferred_element_type=jnp.float32)
    for tile in range(4):
        kept[tile] = screened[:, tile * 128 : tile * 128 + 128]
        virtual[tile] = product[:, tile * 128 : tile * 128 + 128]
    for which, source in enumerate((kept, virtual)):
        for tile in range(4):
            even = source[tile, pl.ds(0, 128, stride=2), :]
            odd = source[tile, pl.ds(1, 128, stride=2), :]
            for half in range(2):
                cut = slice(half * 64, half * 64 + 64)
                block = jnp.concatenate([even[:, cut], odd[:, cut]], axis=1).astype(jnp.bfloat16)
                for w in range(8):
                    dest = w // 2 * 16 + (tile * 2 + half) * 2 + w % 2
                    out_ref[dest, which * 16 : which * 16 + 16, :] = block[w * 16 : w * 16 + 16, :]


def prepare(screen, integrals, virt_density):
    vmem = pl.BlockSpec(memory_space=pltpu.VMEM)
    return pl.pallas_call(
        prepare_kernel,
        out_shape=jax.ShapeDtypeStruct((64, 32, 128), jnp.bfloat16),
        in_specs=[pl.BlockSpec(memory_space=pltpu.SMEM), vmem, vmem],
        out_specs=vmem,
        scratch_shapes=[pltpu.VMEM((4, 256, 128), jnp.float32), pltpu.VMEM((4, 256, 128), jnp.float32)],
        compiler_params=pltpu.CompilerParams(vmem_limit_bytes=8 * 1024 * 1024),
    )(screen, integrals.reshape(256, 512), virt_density)


def unpack(got):
    return got.reshape(4, 16, 16, 128).transpose(0, 2, 1, 3).reshape(64, 2048)


def multiply_kernel(where_ref, *refs):
    columns, mine, other, (out_ref, left, right, done) = refs[:8], refs[8], refs[9], refs[10:]
    y, core = where_ref[0], where_ref[1]
    copies = []

    def bring(source, target):
        copies.append(pltpu.make_async_copy(source, target, done.at[len(copies)]))
        copies[-1].start()

    sign = 1 - 2 * core
    for i, steps in enumerate((0, 1, 2, 3, -1, -2, -3, 4)):
        at = lax.rem(y - sign * steps + 8, 8)
        bring(columns[i], left.at[pl.ds(pl.multiple_of(at * 64, 64), 64), :])
    for i in range(4):
        for blocks, owner in ((mine, core), (other, 1 - core)):
            at = i // 2 * 4 + owner * 2 + i % 2
            bring(blocks.at[i], right.at[:, pl.ds(pl.multiple_of(at * 16, 16), 16), :])
    for copy in copies:
        copy.wait()
    for part_id in range(2):
        part = lax.dot_general(
            left[part_id * 256 : part_id * 256 + 256, :],
            right[...].reshape(512, 2048),
            (((1,), (1,)), ((), ())),
            preferred_element_type=jnp.float32,
        ).astype(jnp.bfloat16)
        for y_column in range(4):
            for x_lo_q in range(2):
                for group in range(4):
                    row = y_column * 64 + x_lo_q * 32
                    dest = group * 16 + (x_lo_q * 4 + part_id * 2 + y_column // 2) * 2 + y_column % 2
                    out_ref[dest] = part[row : row + 32, group * 128 : group * 128 + 128]


def multiply(where, columns, mine, other):
    return pl.pallas_call(
        multiply_kernel,
        out_shape=jax.ShapeDtypeStruct((64, 32, 128), jnp.bfloat16),
        in_specs=[pl.BlockSpec(memory_space=pltpu.SMEM)] + [pl.BlockSpec(memory_space=pl.ANY)] * 10,
        out_specs=pl.BlockSpec(memory_space=pltpu.VMEM),
        scratch_shapes=[
            pltpu.VMEM((512, 2048), jnp.bfloat16),
            pltpu.VMEM((4, 128, 2048), jnp.bfloat16),
            pltpu.SemaphoreType.DMA((16,)),
        ],
        compiler_params=pltpu.CompilerParams(vmem_limit_bytes=20 * 1024 * 1024),
        cost_estimate=pl.CostEstimate(flops=2 * 512 * 512 * 2048, bytes_accessed=4 << 20, transcendentals=0),
    )(where, *columns, mine.reshape(4, 4, 16, 2048), other.reshape(4, 4, 16, 2048))


def finish_kernel(tiles_ref, out_ref):
    for core_q in range(2):
        rows = pl.ds(core_q * 16, 16)
        parts = []
        for w in range(8):
            total = None
            for z in range(8):
                part = tiles_ref[w // 2 * 16 + z * 2 + w % 2, rows, :].astype(jnp.float32)
                total = part if total is None else total + part
            parts.append(total)
        out_ref[:, core_q * 128 : core_q * 128 + 128] = jnp.concatenate(parts, axis=0).T


def finish(tiles):
    vmem = pl.BlockSpec(memory_space=pltpu.VMEM)
    return pl.pallas_call(
        finish_kernel,
        out_shape=jax.ShapeDtypeStruct((128, 256), jnp.float32),
        in_specs=[vmem],
        out_specs=vmem,
        compiler_params=pltpu.CompilerParams(vmem_limit_bytes=8 * 1024 * 1024),
    )(tiles)


def body(integrals, occ_density, virt_density, screen):
    got = lax.all_to_all(prepare(screen, integrals, virt_density), PLANE, 0, 0, tiled=True)
    own = unpack(got[:, :16])
    core = lax.axis_index("core")
    up1 = lax.ppermute(own, ("y", "core"), ring(1))
    down1 = lax.ppermute(own, ("y", "core"), ring(-1))
    up2 = lax.ppermute(own, ("y", "core"), ring(2))
    down2 = lax.ppermute(own, ("y", "core"), ring(-2))
    up3 = lax.ppermute(up2, ("y", "core"), ring(1))
    down3 = lax.ppermute(down2, ("y", "core"), ring(-1))
    far = lax.ppermute(up2, ("y", "core"), ring(2))
    columns = [own, up1, up2, up3, down1, down2, down3, far]
    virt_rows = unpack(got[:, 16:]).reshape(64, 32, 64)
    occupied = jnp.einsum("pms,ml->pls", virt_rows, occ_density, preferred_element_type=jnp.float32)
    occupied = lax.optimization_barrier(occupied.astype(jnp.bfloat16).reshape(64, 2048))
    mine = lax.all_to_all(jnp.broadcast_to(occupied, (4, 64, 2048)), XX, 0, 0, tiled=True)
    other = lax.ppermute(mine, "core", [(0, 1), (1, 0)])
    where = jnp.stack([lax.axis_index("y"), core]).astype(jnp.int32)
    tiles = multiply(where, columns, mine, other)
    got = lax.all_to_all(tiles, PLANE, 0, 0, tiled=True)
    return finish(got)


def solution(mesh):
    fine = Mesh(mesh.devices.reshape(2, 8, 2, 8, 2), AUX + PAIR)
    placed = (P(AUX, PAIR, None), P(), P(), P(AUX, PAIR))

    return jax.shard_map(body, mesh=fine, in_specs=placed, out_specs=P(AUX, PAIR), check_vma=False)
```
